32 devices in a mesh: vir: 8 (over y, x, core), occ: 4 (over z).
Axes of the slice: x: 2, y: 2, z: 4, core: 2. Of those that a mesh axis runs over, the one named last changes fastest.
Arguments:
- perturbation: float32 [10240, 1024], P('vir', 'occ'), may hold values from -6 to 6
- eig_virtual: float32 [10240, 10240], P('vir', 'occ'), may hold values from -0.0625 to 0.0625
- eig_occupied: float32 [1024, 1024], P('occ'), may hold values from -0.1875 to 0.1875
- energy_virtual: float32 [10240], P('occ'), may hold values from 0.5 to 4
- energy_occupied: float32 [1024], replicated, may hold values from -4 to -0.5
Outputs:
- response: float32 [10240, 1024], P('vir', 'occ')
The draws below stay inside these ranges and needn't reach their ends.
All inputs are finite; a program needn't handle non-finite values.
Results may differ from the reference program's by a relative error of at most 0.000078.
Values sent between devices are 32-bit elements; how exact they have to be, the bound alone decides.
No kernel may reach another device: no remote copies, remote signals or barrier semaphores. Data moves between devices by JAX's collectives and lax.ppermute only.
A program may use at most 128 MiB of HBM per device.

```python
import math
import jax
import jax.numpy as jnp
from jax import lax

NV = 10240
NO = 1024


def steps_of(own_key, dims, split, smallest, top_value):
    level, own = 1.0, jax.random.fold_in(own_key, 6)
    for position, blocks in split:
        steps = jnp.exp(jax.random.uniform(jax.random.fold_in(own, position), (blocks,), jnp.float32, smallest / len(split), top_value / len(split)))
        level = level * jnp.repeat(steps, dims[position] // blocks).reshape([-1 if axis == position else 1 for axis in range(len(dims))])
    return level


def scatter_about(stream_key, shape, deviation, reach, shards=(), dtype=jnp.bfloat16):
    level = steps_of(stream_key, shape, shards, -0.22, 0.18) if shards else 1.0
    drawn = jax.random.normal(stream_key, shape, jnp.float32) * deviation * level
    return jnp.minimum(jnp.maximum(drawn, -reach), reach).astype(dtype)


def setup_inputs(seed: int = 0) -> dict:
    seeds = jax.random.split(jax.random.key(seed), 6)
    return {
        "perturbation": scatter_about(seeds[0], (NV, NO), 1.0, 6.0, ((0, 8), (1, 4)), jnp.float32),
        "eig_virtual": scatter_about(seeds[1], (NV, NV), NV ** -0.5, 0.0625, ((0, 8), (1, 4)), jnp.float32),
        "eig_occupied": scatter_about(seeds[2], (NO, NO), NO ** -0.5, 0.1875, ((0, 4),), jnp.float32),
        "energy_virtual": jnp.clip(jnp.exp(math.log(4.0) - 2.0794415 * jax.random.uniform(seeds[3], (NV,), jnp.float32) ** steps_of(seeds[3], (NV,), ((0, 4),), -0.2, 0.2)), 0.5, 4.0),
        "energy_occupied": jnp.clip(jax.random.uniform(seeds[4], (NO,), jnp.float32, -4.0, -0.5), -4.0, -0.5),
    }


def reference(perturbation, eig_virtual, eig_occupied, energy_virtual, energy_occupied):
    exact = lax.Precision.HIGHEST
    mixed_rows = jnp.dot(perturbation, eig_occupied, precision=exact, preferred_element_type=jnp.float32)
    projected = jnp.dot(eig_virtual.T, mixed_rows, precision=exact, preferred_element_type=jnp.float32)
    scaled = projected / (energy_virtual[:, None] - energy_occupied[None, :])
    expanded = jnp.dot(eig_virtual, scaled, precision=exact, preferred_element_type=jnp.float32)
    return jnp.dot(expanded, eig_occupied.T, precision=exact, preferred_element_type=jnp.float32)
```

```python
import jax
import jax.numpy as jnp
from jax import lax
from jax.sharding import PartitionSpec as P

SPLIT = (4, 4, 4, 4)


def product(left, right, left_dim, right_dim):
    return lax.dot_general(
        left,
        right,
        (((left_dim,), (right_dim,)), ((), ())),
        precision=lax.Precision.HIGH,
        preferred_element_type=jnp.float32,
    )


def chunk_bounds(width, parts):
    bounds, begin = [], 0
    for part in parts:
        bounds.append((begin, width // part))
        begin += width // part
    assert begin == width
    return bounds


class Line:
    def __init__(self, axis, size):
        self.axis, self.size, self.half = axis, size, size // 2

    def pairs(self, slot):
        near = [(k, k ^ slot) for k in range(self.size) if abs(k - (k ^ slot)) <= self.half]
        far = [(k ^ slot ^ self.half, k) for k in range(self.size) if abs(k - (k ^ slot)) > self.half]
        return near, far

    def order(self):
        return [1, self.half] + [s for s in range(2, self.size) if s != self.half] if self.half > 1 else [1]

    def gather(self, own):
        slots = {0: own}
        for slot in self.order():
            near, far = self.pairs(slot)
            value = lax.ppermute(own, self.axis, near) if near else None
            if far:
                relayed = lax.ppermute(slots[self.half], self.axis, far)
                value = relayed if value is None else value + relayed
            slots[slot] = value
        return [slots[s] for s in range(self.size)]

    def scatter(self, slots):
        slots = list(slots)
        for slot in range(1, self.size):
            near, far = self.pairs(slot)
            if far:
                slots[self.half] = slots[self.half] + lax.ppermute(slots[slot], self.axis, [(b, a) for a, b in far])
        total = slots[0]
        for slot in self.order():
            near, far = self.pairs(slot)
            if near:
                total = total + lax.ppermute(slots[slot], self.axis, [(b, a) for a, b in near])
        return total


class Cube:
    def __init__(self, axis, size):
        self.axis, self.size = axis, size
        bits = [1 << b for b in range(size.bit_length() - 1)]
        self.orders = (bits, bits[:1] + bits[1:][::-1])
        self.stages = len(bits)

    def pairs(self, stage):
        return [(v, v ^ self.orders[v & 1][stage]) for v in range(self.size)]

    def bit(self, stage):
        v = lax.axis_index(self.axis)
        mask = jnp.where(v & 1, self.orders[1][stage], self.orders[0][stage])
        return ((v & mask) != 0).astype(jnp.int32)

    def block(self):
        index = 0
        for stage in range(self.stages):
            index = index * 2 + self.bit(stage)
        return index

    def scatter(self, value, axis):
        for stage in range(self.stages):
            half, bit = value.shape[axis] // 2, self.bit(stage)
            sent = lax.dynamic_slice_in_dim(value, (1 - bit) * half, half, axis)
            kept = lax.dynamic_slice_in_dim(value, bit * half, half, axis)
            value = kept + lax.ppermute(sent, self.axis, self.pairs(stage))
        return value

    def gather(self, value, axis):
        for stage in reversed(range(self.stages)):
            bit = self.bit(stage) == 1
            other = lax.ppermute(value, self.axis, self.pairs(stage))
            value = jnp.concatenate([jnp.where(bit, other, value), jnp.where(bit, value, other)], axis)
        return value


def body(perturbation, eig_virtual, eig_occupied, energy_virtual, energy_occupied):
    line = Line("occ", lax.axis_size("occ"))
    cube = Cube("vir", lax.axis_size("vir"))
    block = cube.block()
    columns = perturbation.shape[1]
    share = eig_virtual.shape[1] // cube.size

    piece = eig_occupied.shape[0] // cube.size
    own_piece = lax.dynamic_slice_in_dim(eig_occupied, block * piece, piece, 0)
    vectors = cube.gather(jnp.stack(line.gather(own_piece)), 1)

    across = perturbation.T
    coarse = []
    bounds = chunk_bounds(columns, SPLIT)
    projected = 0.0
    mixers = []
    for begin, width in bounds:
        whole = jnp.concatenate(line.gather(across[begin : begin + width]), 0)
        part = cube.scatter(product(eig_virtual, whole, 0, 1), 0)
        mixer = vectors[:, begin : begin + width].reshape(-1, vectors.shape[2])
        mixers.append(mixer)
        projected = projected + product(part, mixer, 1, 0)
    own_energy = lax.dynamic_slice_in_dim(energy_virtual, block * share, share, 0)
    scaled = projected / (own_energy[:, None] - energy_occupied[None, :])
    result = [None] * len(bounds)
    for n in reversed(range(len(bounds))):
        width = bounds[n][1]
        gathered = cube.gather(product(scaled, mixers[n], 1, 1), 0)
        spread = product(gathered, eig_virtual, 0, 1)
        result[n] = line.scatter([spread[s * width : (s + 1) * width] for s in range(line.size)])
    return jnp.concatenate(result, 0).T


def solution(mesh):
    in_specs = (P("vir", "occ"), P("vir", "occ"), P("occ", None), P("occ"), P())
    out_specs = P("vir", "occ")
    return jax.shard_map(body, mesh=mesh, in_specs=in_specs, out_specs=out_specs, check_vma=False)
```
